256 devices in a mesh: gx: 16 (over z_hi, x, core), gy: 16 (over z_lo, y).
Axes of the slice: x: 4, y: 4, z: 8 (z_hi: 2, z_lo: 4; z = z_hi * 4 + z_lo), core: 2. Of those that a mesh axis runs over, the one named last changes fastest.
Arguments:
- intensity: float32 [32, 2048, 2048], P(None, 'gx', 'gy'), may hold values from -6 to 6
- weight: float32 [32, 2048, 2048], P(None, 'gx', 'gy'), may hold values from 0.2 to 5
- spacing: int32 [3], replicated, may hold values from 10 to 12
- anchor: int32 [3], replicated, may hold values from 0 to 5
- reach: int32 [1], replicated, may hold values from 36 to 49
Outputs:
- delta_pdf: float32 [32, 2048, 2048], P('gx', 'gy')
The draws below stay inside these ranges and needn't reach their ends.
All inputs are finite; a program needn't handle non-finite values.
Results may differ from the reference program's by a relative error of at most 0.00007.
Values sent between devices are 32-bit elements; how exact they have to be, the bound alone decides.
A program may use at most 128 MiB of HBM per device.

```python
import math
import jax
import jax.numpy as jnp
from jax import lax

NZ = 32
NX = 2048
NY = 2048


def block_scale(own_key, dims, pieces, smallest, largest):
    def one(axis_at, shards_of):
        draws = jax.random.uniform(jax.random.fold_in(jax.random.fold_in(own_key, 6), axis_at), (shards_of,), jnp.float32, smallest / len(pieces), largest / len(pieces))
        return jnp.repeat(jnp.exp(draws), dims[axis_at] // shards_of).reshape((-1,) + (1,) * (len(dims) - axis_at - 1))

    gain = one(*pieces[0])
    for cut in pieces[1:]:
        gain = gain * one(*cut)
    return gain


def centred(key, dims, deviation, limit, split=(), kind=jnp.bfloat16):
    result = deviation * jax.random.normal(key, dims, jnp.float32)
    if split:
        result = result * block_scale(key, dims, split, -0.22, 0.18)
    return jnp.clip(result, -limit, limit).astype(kind)


def setup_inputs(seed: int = 0) -> dict:
    key_of = jax.random.split(jax.random.key(seed), 6)
    intensity = centred(key_of[0], (NZ, NX, NY), 1.0, 6.0, ((1, 16), (2, 16)), jnp.float32)
    weight = jnp.clip(jnp.exp(math.log(5.0) - 3.218876 * jax.random.uniform(key_of[1], (NZ, NX, NY), jnp.float32) ** block_scale(key_of[1], (NZ, NX, NY), ((1, 16), (2, 16)), -0.2, 0.2)), 0.2, 5.0)
    spacing = jax.random.randint(key_of[2], (3,), 10, 13).astype(jnp.int32)
    anchor = jax.random.randint(key_of[3], (3,), 0, 6).astype(jnp.int32)
    reach = jax.random.randint(key_of[4], (1,), 36, 50).astype(jnp.int32)
    return {"intensity": intensity, "weight": weight, "spacing": spacing, "anchor": anchor, "reach": reach}


taps_coef = ((1.0, 2.0, 1.0), (2.0, 4.0, 2.0), (1.0, 2.0, 1.0))

def plane_dist(position, spacing, anchor):
    offset = jnp.mod(position - anchor, spacing)
    return jnp.minimum(offset, spacing - offset)

def punch_holes(zpos, xpos, ypos, spacing, anchor, reach, limit_x, limit_y):
    dist_z = plane_dist(zpos, spacing[0], anchor[0])
    dist_x = plane_dist(xpos, spacing[1], anchor[1])
    dist_y = plane_dist(ypos, spacing[2], anchor[2])
    plane = (dist_x * dist_x)[:, None] + (dist_y * dist_y)[None, :]
    inside_x = (xpos >= 0) & (xpos < limit_x)
    inside_y = (ypos >= 0) & (ypos < limit_y)
    flat = (plane <= reach[0]) & inside_x[:, None] & inside_y[None, :]
    return (dist_z <= 1)[:, None, None] & flat[None, :, :]

def sweep(values_ext, weight_ext, holes):
    size_x = values_ext.shape[1] - 2
    size_y = values_ext.shape[2] - 2
    weighted = None
    total_weight = None
    for row_off in range(3):
        for col_off in range(3):
            near_weight = taps_coef[row_off][col_off] * weight_ext[:, row_off:row_off + size_x, col_off:col_off + size_y]
            term = near_weight * values_ext[:, row_off:row_off + size_x, col_off:col_off + size_y]
            weighted = term if weighted is None else weighted + term
            total_weight = near_weight if total_weight is None else total_weight + near_weight
    centre = values_ext[:, 1:1 + size_x, 1:1 + size_y]
    return jnp.where(holes, weighted / jnp.where(holes, total_weight, 1.0), centre)

def cosine_rows(start, count, length):
    freq = start + jnp.arange(count, dtype=jnp.int32)
    place = 2 * jnp.arange(length, dtype=jnp.int32) + 1
    phase = jnp.mod(freq[:, None] * place[None, :], 4 * length).astype(jnp.float32)
    return jnp.cos(phase * (math.pi / (2 * length))) * math.sqrt(2.0 / length)

def reference(intensity, weight, spacing, anchor, reach):
    holes = punch_holes(jnp.arange(NZ, dtype=jnp.int32), jnp.arange(NX, dtype=jnp.int32), jnp.arange(NY, dtype=jnp.int32), spacing, anchor, reach, NX, NY)
    values = jnp.where(holes, 0.0, intensity)
    pad_width = ((0, 0), (1, 1), (1, 1))
    weight_ext = jnp.pad(weight, pad_width)
    for level in range(3):
        values = sweep(jnp.pad(values, pad_width), weight_ext, holes)
    spectrum_x = jnp.einsum('kx,zxy->zky', cosine_rows(0, NX, NX), values, precision=lax.Precision.HIGHEST)
    return jnp.einsum('zxy,ky->zxk', spectrum_x, cosine_rows(0, NY, NY), precision=lax.Precision.HIGHEST)
```

```python
import functools

import jax
import jax.numpy as jnp
import ml_dtypes
import numpy as np
from jax import lax
from jax.experimental import pallas as pl
from jax.experimental.pallas import tpu as pltpu
from jax.sharding import PartitionSpec as P

MESH = pl.DeviceIdType.MESH
T = 128
EXT = T + 16


def cosine_matrix(length):
    k = np.arange(length, dtype=np.int64)
    phase = (k[:, None] * (2 * k[None, :] + 1)) % (4 * length)
    return np.cos(phase * (np.pi / (2 * length))) * np.sqrt(2.0 / length)


def split_pair(matrix):
    matrix = matrix.astype(np.float32)
    high = matrix.astype(ml_dtypes.bfloat16)
    low = (matrix - high.astype(np.float32)).astype(ml_dtypes.bfloat16)
    return high, low


def xor(a, b, bits):
    total = 0
    for i in range(bits):
        total = total + (2**i) * ((a // 2**i + b // 2**i) % 2)
    return total


def high_low(x):
    high = x.astype(jnp.bfloat16)
    return high, (x - high.astype(jnp.float32)).astype(jnp.bfloat16)


def plane_dist(position, spacing, anchor):
    offset = position - anchor
    offset = offset - spacing * jnp.floor((offset + 0.5) / spacing)
    return jnp.minimum(offset, spacing - offset)


def kernel(
    nx, ny, depth,
    i_hbm, w_hbm, sp_ref, an_ref, re_ref, chi_hbm, clo_hbm, thi_hbm, tlo_hbm,
    out_hbm,
    iv, wv, fbuf, xpack, xrecv, ypack, yrecv, flat, inside,
    recv1, fx, sbuf, recv2, acc, chi, clo, thi, tlo,
    lsem, csem, osem, hs, hr, s1, r1, s2, r2,
):
    gx = lax.axis_index("gx")
    gy = lax.axis_index("gy")
    full_x, full_y = nx * T, ny * T
    bits_x, bits_y = nx.bit_length() - 1, ny.bit_length() - 1
    left, right = (gy + ny - 1) % ny, (gy + 1) % ny
    up, down = (gx + nx - 1) % nx, (gx + 1) % nx

    loads = [
        pltpu.make_async_copy(i_hbm, iv, lsem.at[0]),
        pltpu.make_async_copy(w_hbm, wv, lsem.at[1]),
    ]
    consts = [
        pltpu.make_async_copy(src, dst, csem.at[i])
        for i, (src, dst) in enumerate(
            ((chi_hbm, chi), (clo_hbm, clo), (thi_hbm, thi), (tlo_hbm, tlo))
        )
    ]
    for cp in loads:
        cp.start()
    barrier = pltpu.get_barrier_semaphore()
    for s in range(1, nx):
        pl.semaphore_signal(barrier, inc=1, device_id=((gx + s) % nx, gy), device_id_type=MESH)
    for s in range(1, ny):
        pl.semaphore_signal(barrier, inc=1, device_id=(gx, (gy + s) % ny), device_id_type=MESH)
    for px in (up, down):
        for py in (left, right):
            pl.semaphore_signal(barrier, inc=1, device_id=(px, py), device_id_type=MESH)
    for cp in consts:
        cp.start()

    lane = lax.broadcasted_iota(jnp.int32, (EXT, T), 1)
    row = lax.broadcasted_iota(jnp.int32, (EXT, T), 0)
    xpos = gx * T - 8 + row
    in_x = (xpos >= 0) & (xpos < full_x)
    dist_x = plane_dist(
        xpos.astype(jnp.float32), sp_ref[1].astype(jnp.float32), an_ref[1].astype(jnp.float32)
    )
    for part in range(2):
        if part == 0:
            ypos = gy * T + lane
            keep = in_x
        else:
            ypos = gy * T + jnp.where(lane < T // 2, lane + T, lane - T)
            keep = in_x & (ypos >= 0) & (ypos < full_y) & ((lane < 4) | (lane >= T - 4))
        dist_y = plane_dist(
            ypos.astype(jnp.float32), sp_ref[2].astype(jnp.float32), an_ref[2].astype(jnp.float32)
        )
        hole = dist_x * dist_x + dist_y * dist_y <= re_ref[0].astype(jnp.float32)
        inside[part] = jnp.where(keep, 1.0, 0.0)
        flat[part] = jnp.where(keep & hole, 1.0, 0.0)

    for cp in loads:
        cp.wait()

    sub = lax.broadcasted_iota(jnp.int32, (8, T), 0)
    tile_lane = lax.broadcasted_iota(jnp.int32, (T, T), 1)
    ypack[...] = jnp.zeros_like(ypack)

    @pl.loop(0, depth // 4)
    def _(q):
        for arr, src in enumerate((iv, wv)):
            first = ypack[0, arr]
            second = ypack[1, arr]
            for j in range(4):
                layer = 4 * q + j
                tile = src[layer]
                mine = tile_lane // 4 == layer
                first = jnp.where(mine, pltpu.roll(tile, (4 * layer + 4) % T, 1), first)
                second = jnp.where(mine, pltpu.roll(tile, (4 * layer) % T, 1), second)
            ypack[0, arr] = first
            ypack[1, arr] = second
            for j in range(2):
                even, odd = src.at[4 * q + 2 * j], src.at[4 * q + 2 * j + 1]
                xpack[0, arr, 2 * q + j] = jnp.where(
                    sub < 4, even[0:8], pltpu.roll(odd[0:8], 4, 0)
                )
                xpack[1, arr, 2 * q + j] = jnp.where(
                    sub >= 4, even[T - 8 : T], pltpu.roll(odd[T - 8 : T], 4, 0)
                )

    pl.semaphore_wait(barrier, (nx - 1) + (ny - 1) + 4)

    halo = []
    routes = (
        (ypack.at[0], yrecv.at[0, :, pl.ds(8, T)], (gx, right)),
        (ypack.at[1], yrecv.at[1, :, pl.ds(8, T)], (gx, left)),
        (xpack.at[0], xrecv.at[1], (up, gy)),
        (xpack.at[1], xrecv.at[0], (down, gy)),
        (ypack.at[0, :, pl.ds(T - 8, 8)], yrecv.at[0, :, pl.ds(0, 8)], (down, right)),
        (ypack.at[0, :, pl.ds(0, 8)], yrecv.at[0, :, pl.ds(T + 8, 8)], (up, right)),
        (ypack.at[1, :, pl.ds(T - 8, 8)], yrecv.at[1, :, pl.ds(0, 8)], (down, left)),
        (ypack.at[1, :, pl.ds(0, 8)], yrecv.at[1, :, pl.ds(T + 8, 8)], (up, left)),
    )
    for i, (src, dst, dev) in enumerate(routes):
        cp = pltpu.make_async_remote_copy(
            src_ref=src, dst_ref=dst, send_sem=hs.at[i], recv_sem=hr.at[i],
            device_id=dev, device_id_type=MESH,
        )
        cp.start()
        halo.append(cp)
    for cp in halo:
        cp.wait()

    def blur(main, side):
        def across(a, b):
            before = pltpu.roll(jnp.where(lane == T - 1, b, a), 1, 1)
            after = pltpu.roll(jnp.where(lane == 0, b, a), T - 1, 1)
            s = (before + after) + (a + a)
            return (pltpu.roll(s, 1, 0) + pltpu.roll(s, EXT - 1, 0)) + (s + s)

        return across(main, side), across(side, main)

    def extended(arr, src, layer, half):
        top, bottom = xrecv[0, arr, layer // 2], xrecv[1, arr, layer // 2]
        if half:
            top, bottom = pltpu.roll(top, 4, 0), pltpu.roll(bottom, 4, 0)
        main = jnp.concatenate([top, src[layer], bottom], axis=0)
        before = pltpu.roll(yrecv[0, arr], (2 * T - 4 - 4 * layer) % T, 1)
        after = pltpu.roll(yrecv[1, arr], (T - 4 * layer) % T, 1)
        return main, jnp.where(lane < T // 2, after, before)

    def fill(layer, half):
        zpos = lax.broadcasted_iota(jnp.int32, (1, T), 0) + layer
        dist_z = plane_dist(
            zpos.astype(jnp.float32), sp_ref[0].astype(jnp.float32), an_ref[0].astype(jnp.float32)
        )
        zflag = jnp.where(dist_z <= 1.0, 1.0, 0.0)
        holes = [flat[part] * zflag > 0.5 for part in range(2)]
        weights = [w * inside[part] for part, w in enumerate(extended(1, wv, layer, half))]
        values = [
            jnp.where(h, 0.0, v) for h, v in zip(holes, extended(0, iv, layer, half))
        ]
        inverse = [
            1.0 / jnp.where(h, d, 1.0) for h, d in zip(holes, blur(*weights))
        ]
        for _ in range(3):
            numer = blur(*[w * v for w, v in zip(weights, values)])
            values = [
                jnp.where(h, n * r, v) for h, n, r, v in zip(holes, numer, inverse, values)
            ]
        fbuf[layer] = values[0][8 : 8 + T]

    def first_copy(layer, half, peer):
        return pltpu.make_async_remote_copy(
            src_ref=fbuf.at[layer], dst_ref=recv1.at[gx, half],
            send_sem=s1.at[layer], recv_sem=r1.at[gx, half],
            device_id=(peer, gy), device_id_type=MESH,
        )

    for half in range(2):
        @pl.loop(0, nx - 1)
        def _(t):
            peer = xor(gx, nx - 1 - t, bits_x)
            layer = 2 * peer + half
            fill(layer, half)
            first_copy(layer, half, peer).start()

    for half in range(2):
        fill(2 * gx + half, half)
        recv1[gx, half] = fbuf[2 * gx + half]

    def second_copy(half, block):
        return pltpu.make_async_remote_copy(
            src_ref=sbuf.at[half, block], dst_ref=recv2.at[gy, half],
            send_sem=s2.at[half, block], recv_sem=r2.at[gy, half],
            device_id=(gx, block), device_id_type=MESH,
        )

    groups = ny // 4
    order = [o for o in (2, 3, 1, 0) if o < groups]
    for half in range(2):
        @pl.loop(0, nx)
        def _(t):
            peer = xor(gx, t, bits_x)

            @pl.when(t > 0)
            def _():
                pltpu.make_async_remote_copy(
                    src_ref=fbuf.at[0], dst_ref=recv1.at[peer, half],
                    send_sem=s1.at[0], recv_sem=r1.at[peer, half],
                    device_id=(peer, gy), device_id_type=MESH,
                ).wait_recv()

            high, low = high_low(recv1[peer, half])
            start = pl.multiple_of(peer * T, T)
            fx[pl.ds(start, T), 0:T] = high
            fx[pl.ds(start, T), T : 2 * T] = low

        if half == 0:
            for cp in consts[:2]:
                cp.wait()
        for o in order:
            group = xor(gy // 4, o, bits_y - 2)
            start = pl.multiple_of(group * (4 * T), 4 * T)
            both = jnp.dot(
                chi[pl.ds(start, 4 * T), :], fx[...], preferred_element_type=jnp.float32
            )
            rest = jnp.dot(
                clo[pl.ds(start, 4 * T), :], fx[:, 0:T], preferred_element_type=jnp.float32
            )
            total = both[:, 0:T] + (both[:, T : 2 * T] + rest)
            for j in range(4):
                block = 4 * group + j
                sbuf[half, block] = total[j * T : (j + 1) * T]

                @pl.when(block != gy)
                def _():
                    second_copy(half, block).start()

                @pl.when(block == gy)
                def _():
                    recv2[gy, half] = sbuf[half, block]

    for cp in consts[2:]:
        cp.wait()
    outs = []
    for half in range(2):
        for o in range(groups):
            group = xor(gy // 4, o, bits_y - 2)
            parts = []
            for j in range(4):
                block = 4 * group + j

                @pl.when(block != gy)
                def _():
                    pltpu.make_async_remote_copy(
                        src_ref=sbuf.at[half, 0], dst_ref=recv2.at[block, half],
                        send_sem=s2.at[half, 0], recv_sem=r2.at[block, half],
                        device_id=(gx, block), device_id_type=MESH,
                    ).wait_recv()

                parts.append(recv2[block, half])
            high, low = high_low(jnp.concatenate(parts, axis=1))
            stacked = jnp.concatenate([high, low], axis=0)
            start = pl.multiple_of(group * (4 * T), 4 * T)

            @pl.loop(0, full_y // 512)
            def _(c):
                cols = pl.ds(pl.multiple_of(c * 512, 512), 512)
                both = jnp.dot(
                    stacked, thi[pl.ds(start, 4 * T), cols], preferred_element_type=jnp.float32
                )
                rest = jnp.dot(
                    high, tlo[pl.ds(start, 4 * T), cols], preferred_element_type=jnp.float32
                )
                total = both[0:T] + (both[T : 2 * T] + rest)
                if o == 0:
                    acc[half, :, cols] = total
                else:
                    acc[half, :, cols] += total

        cp = pltpu.make_async_copy(acc.at[half], out_hbm.at[half], osem.at[half])
        cp.start()
        outs.append(cp)

    for half in range(2):
        @pl.loop(0, nx - 1)
        def _(t):
            peer = xor(gx, nx - 1 - t, bits_x)
            first_copy(2 * peer + half, half, peer).wait_send()

        @pl.loop(1, ny)
        def _(t):
            second_copy(half, xor(gy, t, bits_y)).wait_send()
    for cp in outs:
        cp.wait()


def per_device(nx, ny, intensity, weight, spacing, anchor, reach):
    depth = intensity.shape[0]
    full_x, full_y = nx * T, ny * T
    chi, clo = split_pair(cosine_matrix(full_x))
    thi, tlo = split_pair(cosine_matrix(full_y).T)
    f32, bf16 = jnp.float32, jnp.bfloat16
    vmem, dma = pltpu.VMEM, pltpu.SemaphoreType.DMA
    anywhere = pl.BlockSpec(memory_space=pl.ANY)
    scalars = pl.BlockSpec(memory_space=pltpu.SMEM)
    return pl.pallas_call(
        functools.partial(kernel, nx, ny, depth),
        out_shape=jax.ShapeDtypeStruct((2, T, full_y), f32),
        in_specs=[anywhere] * 2 + [scalars] * 3 + [anywhere] * 4,
        out_specs=anywhere,
        scratch_shapes=[
            vmem((depth, T, T), f32),
            vmem((depth, T, T), f32),
            vmem((depth, T, T), f32),
            vmem((2, 2, depth // 2, 8, T), f32),
            vmem((2, 2, depth // 2, 8, T), f32),
            vmem((2, 2, T, T), f32),
            vmem((2, 2, EXT, T), f32),
            vmem((2, EXT, T), f32),
            vmem((2, EXT, T), f32),
            vmem((nx, 2, T, T), f32),
            vmem((full_x, 2 * T), bf16),
            vmem((2, ny, T, T), f32),
            vmem((ny, 2, T, T), f32),
            vmem((2, T, full_y), f32),
            vmem((full_x, full_x), bf16),
            vmem((full_x, full_x), bf16),
            vmem((full_y, full_y), bf16),
            vmem((full_y, full_y), bf16),
            dma((2,)), dma((4,)), dma((2,)), dma((8,)), dma((8,)),
            dma((depth,)), dma((nx, 2)), dma((2, ny)), dma((ny, 2)),
        ],
        compiler_params=pltpu.CompilerParams(
            collective_id=0, has_side_effects=True, vmem_limit_bytes=60 * 2**20
        ),
    )(intensity, weight, spacing, anchor, reach, chi, clo, thi, tlo)


def solution(mesh):
    nx, ny = mesh.shape["gx"], mesh.shape["gy"]
    in_specs = (P(None, "gx", "gy"), P(None, "gx", "gy"), P(), P(), P())
    return jax.shard_map(
        functools.partial(per_device, nx, ny),
        mesh=mesh, in_specs=in_specs, out_specs=P("gx", "gy", None), check_vma=False,
    )
```

```python
import functools

import jax
import jax.numpy as jnp
import ml_dtypes
import numpy as np
from jax import lax
from jax.experimental import pallas as pl
from jax.experimental.pallas import tpu as pltpu
from jax.sharding import PartitionSpec as P

MESH = pl.DeviceIdType.MESH
T = 128
EXT = T + 16


def cosine_matrix(length):
    k = np.arange(length, dtype=np.int64)
    phase = (k[:, None] * (2 * k[None, :] + 1)) % (4 * length)
    return np.cos(phase * (np.pi / (2 * length))) * np.sqrt(2.0 / length)


def split_pair(matrix):
    matrix = matrix.astype(np.float32)
    high = matrix.astype(ml_dtypes.bfloat16)
    low = (matrix - high.astype(np.float32)).astype(ml_dtypes.bfloat16)
    return high, low


def xor(a, b, bits):
    total = 0
    for i in range(bits):
        total = total + (2**i) * ((a // 2**i + b // 2**i) % 2)
    return total


def high_low(x):
    high = x.astype(jnp.bfloat16)
    return high, (x - high.astype(jnp.float32)).astype(jnp.bfloat16)


def plane_dist(position, spacing, anchor):
    offset = position - anchor
    offset = offset - spacing * jnp.floor((offset + 0.5) / spacing)
    return jnp.minimum(offset, spacing - offset)


def hole_slots(depth):
    return 3 * (depth // 10 + 1) + 3 * (depth // 10 + 1) % 2


def kernel(
    nx, ny, depth,
    i_hbm, w_hbm, sp_ref, an_ref, re_ref, chi_hbm, clo_hbm, thi_hbm, tlo_hbm,
    out0_hbm, out1_hbm,
    iv, wv, fbuf, xpack, xrecv, ypack, yrecv, flat, inside,
    recv1, fx, sbuf, recv2, acc, chi, clo, thi, tlo,
    lsem, csem, osem, hs, hr, s1, r1, s2, r2,
):
    gx = lax.axis_index("gx")
    gy = lax.axis_index("gy")
    full_x, full_y = nx * T, ny * T
    slots = hole_slots(depth)
    bits_x, bits_y = nx.bit_length() - 1, ny.bit_length() - 1
    left, right = (gy + ny - 1) % ny, (gy + 1) % ny
    up, down = (gx + nx - 1) % nx, (gx + 1) % nx

    loads = [
        pltpu.make_async_copy(i_hbm, iv, lsem.at[0]),
        pltpu.make_async_copy(w_hbm, wv, lsem.at[1]),
    ]
    consts = [
        pltpu.make_async_copy(src, dst, csem.at[i])
        for i, (src, dst) in enumerate(
            ((chi_hbm, chi), (clo_hbm, clo), (thi_hbm, thi), (tlo_hbm, tlo))
        )
    ]
    for cp in loads:
        cp.start()
    barrier = pltpu.get_barrier_semaphore()
    for s in range(1, nx):
        pl.semaphore_signal(barrier, inc=1, device_id=((gx + s) % nx, gy), device_id_type=MESH)
    for s in range(1, ny):
        pl.semaphore_signal(barrier, inc=1, device_id=(gx, (gy + s) % ny), device_id_type=MESH)
    for px in (up, down):
        for py in (left, right):
            pl.semaphore_signal(barrier, inc=1, device_id=(px, py), device_id_type=MESH)
    for cp in consts:
        cp.start()

    lane = lax.broadcasted_iota(jnp.int32, (EXT, T), 1)
    row = lax.broadcasted_iota(jnp.int32, (EXT, T), 0)
    xpos = gx * T - 8 + row
    in_x = (xpos >= 0) & (xpos < full_x)
    dist_x = plane_dist(
        xpos.astype(jnp.float32), sp_ref[1].astype(jnp.float32), an_ref[1].astype(jnp.float32)
    )
    for part in range(2):
        if part == 0:
            ypos = gy * T + lane
            keep = in_x
        else:
            ypos = gy * T + jnp.where(lane < T // 2, lane + T, lane - T)
            keep = in_x & (ypos >= 0) & (ypos < full_y) & ((lane < 4) | (lane >= T - 4))
        dist_y = plane_dist(
            ypos.astype(jnp.float32), sp_ref[2].astype(jnp.float32), an_ref[2].astype(jnp.float32)
        )
        hole = dist_x * dist_x + dist_y * dist_y <= re_ref[0].astype(jnp.float32)
        inside[part] = jnp.where(keep, 1.0, 0.0)
        flat[part] = jnp.where(keep & hole, 1.0, 0.0)

    for cp in loads:
        cp.wait()

    sub = lax.broadcasted_iota(jnp.int32, (8, T), 0)
    group = lax.broadcasted_iota(jnp.int32, (T, T), 1) // 4
    first = second = jnp.zeros((T, T), jnp.float32)
    for arr, src in enumerate((iv, wv)):
        ends = []
        for slot in range(slots):
            layer = an_ref[0] + (slot // 3) * sp_ref[0] + (slot % 3 - 1)
            tile = src[jnp.clip(layer, 0, depth - 1)]
            place = slot + arr * slots
            first = jnp.where(group == place, pltpu.roll(tile, (4 * place + 4) % T, 1), first)
            second = jnp.where(group == place, pltpu.roll(tile, (4 * place) % T, 1), second)
            ends.append((tile[0:8], tile[T - 8 : T]))
        for pair in range(slots // 2):
            even, odd = ends[2 * pair], ends[2 * pair + 1]
            xpack[0, arr, pair] = jnp.where(sub < 4, even[0], pltpu.roll(odd[0], 4, 0))
            xpack[1, arr, pair] = jnp.where(sub >= 4, even[1], pltpu.roll(odd[1], 4, 0))
    ypack[0] = first
    ypack[1] = second

    pl.semaphore_wait(barrier, (nx - 1) + (ny - 1) + 4)

    has_up, has_down = gx > 0, gx < nx - 1
    has_left, has_right = gy > 0, gy < ny - 1
    ends, starts, rows = pl.ds(T - 8, 8), pl.ds(0, 8), pl.ds(8, T)
    before, after = pl.ds(0, 8), pl.ds(T + 8, 8)
    routes = (
        (ypack.at[0], yrecv.at[0, rows], (gx, right), has_right, has_left),
        (ypack.at[1], yrecv.at[1, rows], (gx, left), has_left, has_right),
        (xpack.at[0], xrecv.at[1], (up, gy), has_up, has_down),
        (xpack.at[1], xrecv.at[0], (down, gy), has_down, has_up),
        (ypack.at[0, ends], yrecv.at[0, before], (down, right), has_down & has_right, has_up & has_left),
        (ypack.at[0, starts], yrecv.at[0, after], (up, right), has_up & has_right, has_down & has_left),
        (ypack.at[1, ends], yrecv.at[1, before], (down, left), has_down & has_left, has_up & has_right),
        (ypack.at[1, starts], yrecv.at[1, after], (up, left), has_up & has_left, has_down & has_right),
    )
    halo = []
    for i, (src, dst, dev, sends, receives) in enumerate(routes):
        cp = pltpu.make_async_remote_copy(
            src_ref=src, dst_ref=dst, send_sem=hs.at[i], recv_sem=hr.at[i],
            device_id=dev, device_id_type=MESH,
        )
        halo.append((cp, sends, receives))
        pl.when(sends)(cp.start)
    for cp, _, receives in halo:
        pl.when(receives)(cp.wait_recv)

    def blur(main, side):
        def across(a, b):
            before = pltpu.roll(jnp.where(lane == T - 1, b, a), 1, 1)
            after = pltpu.roll(jnp.where(lane == 0, b, a), T - 1, 1)
            s = (before + after) + (a + a)
            return (pltpu.roll(s, 1, 0) + pltpu.roll(s, EXT - 1, 0)) + (s + s)

        return across(main, side), across(side, main)

    def extended(arr, src, layer, slot):
        top, bottom = xrecv[0, arr, slot // 2], xrecv[1, arr, slot // 2]
        odd = jnp.full((8, T), slot % 2, jnp.int32) == 1
        top = jnp.where(odd, pltpu.roll(top, 4, 0), top)
        bottom = jnp.where(odd, pltpu.roll(bottom, 4, 0), bottom)
        main = jnp.concatenate([top, src[layer], bottom], axis=0)
        shift = 2 * T - 4 * (slot + arr * slots)
        before = pltpu.roll(yrecv[0], (shift - 4) % T, 1)
        after = pltpu.roll(yrecv[1], shift % T, 1)
        return main, jnp.where(lane < T // 2, after, before)

    def fill(layer):
        place = layer - an_ref[0] + 1
        turn = 0
        for m in range(1, slots // 3):
            turn = turn + (place >= m * sp_ref[0]).astype(jnp.int32)
        slot = 3 * turn + jnp.clip(place - turn * sp_ref[0], 0, 2)
        zpos = lax.broadcasted_iota(jnp.int32, (1, T), 0) + layer
        dist_z = plane_dist(
            zpos.astype(jnp.float32), sp_ref[0].astype(jnp.float32), an_ref[0].astype(jnp.float32)
        )
        zflag = jnp.where(dist_z <= 1.0, 1.0, 0.0)
        masks = [flat[part] * zflag for part in range(2)]
        holes = [m > 0.5 for m in masks]
        weights = [
            jnp.where(inside[part] > 0.5, w, 0.0)
            for part, w in enumerate(extended(1, wv, layer, slot))
        ]
        values = [
            jnp.where(inside[part] - masks[part] > 0.5, v, 0.0)
            for part, v in enumerate(extended(0, iv, layer, slot))
        ]
        inverse = [
            1.0 / jnp.where(h, d, 1.0) for h, d in zip(holes, blur(*weights))
        ]
        for _ in range(3):
            numer = blur(*[w * v for w, v in zip(weights, values)])
            values = [
                jnp.where(h, n * r, v) for h, n, r, v in zip(holes, numer, inverse, values)
            ]
        fbuf[layer] = values[0][8 : 8 + T]

    def first_copy(layer, half, peer):
        return pltpu.make_async_remote_copy(
            src_ref=fbuf.at[layer], dst_ref=recv1.at[gx, half],
            send_sem=s1.at[layer], recv_sem=r1.at[gx, half],
            device_id=(peer, gy), device_id_type=MESH,
        )

    for half in range(2):
        @pl.loop(0, nx - 1)
        def _(t):
            peer = xor(gx, nx - 1 - t, bits_x)
            layer = 2 * peer + half
            fill(layer)
            first_copy(layer, half, peer).start()

    for half in range(2):
        fill(2 * gx + half)
        recv1[gx, half] = fbuf[2 * gx + half]

    def second_copy(half, block):
        return pltpu.make_async_remote_copy(
            src_ref=sbuf.at[half, block], dst_ref=recv2.at[gy, half],
            send_sem=s2.at[half, block], recv_sem=r2.at[gy, half],
            device_id=(gx, block), device_id_type=MESH,
        )

    groups = ny // 4
    order = [o for o in (2, 3, 1, 0) if o < groups]
    for half in range(2):
        @pl.loop(0, nx)
        def _(t):
            peer = xor(gx, t, bits_x)

            @pl.when(t > 0)
            def _():
                pltpu.make_async_remote_copy(
                    src_ref=fbuf.at[0], dst_ref=recv1.at[peer, half],
                    send_sem=s1.at[0], recv_sem=r1.at[peer, half],
                    device_id=(peer, gy), device_id_type=MESH,
                ).wait_recv()

            high, low = high_low(recv1[peer, half])
            start = pl.multiple_of(peer * T, T)
            fx[pl.ds(start, T), 0:T] = high
            fx[pl.ds(start, T), T : 2 * T] = low

        if half == 0:
            for cp in consts[:2]:
                cp.wait()
        for o in order:
            group = xor(gy // 4, o, bits_y - 2)
            start = pl.multiple_of(group * (4 * T), 4 * T)
            both = jnp.dot(
                chi[pl.ds(start, 4 * T), :], fx[...], preferred_element_type=jnp.float32
            )
            rest = jnp.dot(
                clo[pl.ds(start, 4 * T), :], fx[:, 0:T], preferred_element_type=jnp.float32
            )
            total = both[:, 0:T] + (both[:, T : 2 * T] + rest)
            for j in range(4):
                sbuf[half, 4 * group + j] = total[j * T : (j + 1) * T]
            for j in range(4):
                block = 4 * group + xor(gy % 4, j, 2)

                @pl.when(block != gy)
                def _():
                    second_copy(half, block).start()

                @pl.when(block == gy)
                def _():
                    recv2[gy, half] = sbuf[half, block]

    for cp in consts[2:]:
        cp.wait()
    outs = []
    for half in range(2):
        for o in range(groups):
            group = xor(gy // 4, o, bits_y - 2)
            parts = []
            for j in range(4):
                block = 4 * group + j

                @pl.when(block != gy)
                def _():
                    pltpu.make_async_remote_copy(
                        src_ref=sbuf.at[half, 0], dst_ref=recv2.at[block, half],
                        send_sem=s2.at[half, 0], recv_sem=r2.at[block, half],
                        device_id=(gx, block), device_id_type=MESH,
                    ).wait_recv()

                parts.append(recv2[block, half])
            high, low = high_low(jnp.concatenate(parts, axis=1))
            stacked = jnp.concatenate([high, low], axis=0)
            start = pl.multiple_of(group * (4 * T), 4 * T)

            @pl.loop(0, full_y // 512)
            def _(c):
                cols = pl.ds(pl.multiple_of(c * 512, 512), 512)
                both = jnp.dot(
                    stacked, thi[pl.ds(start, 4 * T), cols], preferred_element_type=jnp.float32
                )
                rest = jnp.dot(
                    high, tlo[pl.ds(start, 4 * T), cols], preferred_element_type=jnp.float32
                )
                total = both[0:T] + (both[T : 2 * T] + rest)
                if o == 0:
                    acc[half, :, cols] = total
                else:
                    acc[half, :, cols] += total

        cp = pltpu.make_async_copy(
            acc.at[half], (out0_hbm, out1_hbm)[half].at[0], osem.at[half]
        )
        cp.start()
        outs.append(cp)

    for half in range(2):
        @pl.loop(0, nx - 1)
        def _(t):
            peer = xor(gx, nx - 1 - t, bits_x)
            first_copy(2 * peer + half, half, peer).wait_send()

        @pl.loop(1, ny)
        def _(t):
            second_copy(half, xor(gy, t, bits_y)).wait_send()
    for cp, sends, _ in halo:
        pl.when(sends)(cp.wait_send)
    for cp in outs:
        cp.wait()


def per_device(nx, ny, intensity, weight, spacing, anchor, reach):
    depth = intensity.shape[0]
    full_x, full_y = nx * T, ny * T
    chi, clo = split_pair(cosine_matrix(full_x))
    thi, tlo = split_pair(cosine_matrix(full_y).T)
    f32, bf16 = jnp.float32, jnp.bfloat16
    vmem, dma = pltpu.VMEM, pltpu.SemaphoreType.DMA
    anywhere = pl.BlockSpec(memory_space=pl.ANY)
    scalars = pl.BlockSpec(memory_space=pltpu.SMEM)
    slots = hole_slots(depth)
    first, second = pl.pallas_call(
        functools.partial(kernel, nx, ny, depth),
        out_shape=[jax.ShapeDtypeStruct((1, T, full_y), f32)] * 2,
        in_specs=[anywhere] * 2 + [scalars] * 3 + [anywhere] * 4,
        out_specs=[anywhere] * 2,
        scratch_shapes=[
            vmem((depth, T, T), f32),
            vmem((depth, T, T), f32),
            vmem((depth, T, T), f32),
            vmem((2, 2, slots // 2, 8, T), f32),
            vmem((2, 2, slots // 2, 8, T), f32),
            vmem((2, T, T), f32),
            vmem((2, EXT, T), f32),
            vmem((2, EXT, T), f32),
            vmem((2, EXT, T), f32),
            vmem((nx, 2, T, T), f32),
            vmem((full_x, 2 * T), bf16),
            vmem((2, ny, T, T), f32),
            vmem((ny, 2, T, T), f32),
            vmem((2, T, full_y), f32),
            vmem((full_x, full_x), bf16),
            vmem((full_x, full_x), bf16),
            vmem((full_y, full_y), bf16),
            vmem((full_y, full_y), bf16),
            dma((2,)), dma((4,)), dma((2,)), dma((8,)), dma((8,)),
            dma((depth,)), dma((nx, 2)), dma((2, ny)), dma((ny, 2)),
        ],
        compiler_params=pltpu.CompilerParams(
            collective_id=0, has_side_effects=True, vmem_limit_bytes=60 * 2**20
        ),
    )(intensity, weight, spacing, anchor, reach, chi, clo, thi, tlo)
    return jnp.concatenate([first, second], axis=0)


def solution(mesh):
    nx, ny = mesh.shape["gx"], mesh.shape["gy"]
    in_specs = (P(None, "gx", "gy"), P(None, "gx", "gy"), P(), P(), P())
    return jax.shard_map(
        functools.partial(per_device, nx, ny),
        mesh=mesh, in_specs=in_specs, out_specs=P("gx", "gy", None), check_vma=False,
    )
```

```python
import functools

import jax
import jax.numpy as jnp
import ml_dtypes
import numpy as np
from jax import lax
from jax.experimental import pallas as pl
from jax.experimental.pallas import tpu as pltpu
from jax.sharding import PartitionSpec as P

MESH = pl.DeviceIdType.MESH
T = 128
EXT = T + 16


def cosine_matrix(length):
    k = np.arange(length, dtype=np.int64)
    phase = (k[:, None] * (2 * k[None, :] + 1)) % (4 * length)
    return np.cos(phase * (np.pi / (2 * length))) * np.sqrt(2.0 / length)


def split_pair(matrix):
    matrix = matrix.astype(np.float32)
    high = matrix.astype(ml_dtypes.bfloat16)
    low = (matrix - high.astype(np.float32)).astype(ml_dtypes.bfloat16)
    return high, low


def xor(a, b, bits):
    total = 0
    for i in range(bits):
        total = total + (2**i) * ((a // 2**i + b // 2**i) % 2)
    return total


def high_low(x):
    high = x.astype(jnp.bfloat16)
    return high, (x - high.astype(jnp.float32)).astype(jnp.bfloat16)


def plane_dist(position, spacing, anchor):
    offset = position - anchor
    offset = offset - spacing * jnp.floor((offset + 0.5) / spacing)
    return jnp.minimum(offset, spacing - offset)


def hole_slots(depth):
    return 3 * (depth // 10 + 1) + 3 * (depth // 10 + 1) % 2


def kernel(
    nx, ny, depth,
    i_hbm, w_hbm, sp_ref, an_ref, re_ref, chi_hbm, clo_hbm, thi_hbm, tlo_hbm,
    acc,
    iv, wv, fbuf, xpack, xrecv, ypack, yrecv, flat, inside,
    recv1, fx, sbuf, recv2, chi, clo, thi, tlo,
    lsem, csem, hs, hr, s1, r1, s2, r2,
):
    gx = lax.axis_index("gx")
    gy = lax.axis_index("gy")
    full_x, full_y = nx * T, ny * T
    slots = hole_slots(depth)
    bits_x, bits_y = nx.bit_length() - 1, ny.bit_length() - 1
    left, right = (gy + ny - 1) % ny, (gy + 1) % ny
    up, down = (gx + nx - 1) % nx, (gx + 1) % nx

    loads = [
        pltpu.make_async_copy(i_hbm, iv, lsem.at[0]),
        pltpu.make_async_copy(w_hbm, wv, lsem.at[1]),
    ]
    consts = [
        pltpu.make_async_copy(src, dst, csem.at[i])
        for i, (src, dst) in enumerate(
            ((chi_hbm, chi), (clo_hbm, clo), (thi_hbm, thi), (tlo_hbm, tlo))
        )
    ]
    for cp in loads:
        cp.start()
    barrier = pltpu.get_barrier_semaphore()
    for s in range(1, nx):
        pl.semaphore_signal(barrier, inc=1, device_id=((gx + s) % nx, gy), device_id_type=MESH)
    for s in range(1, ny):
        pl.semaphore_signal(barrier, inc=1, device_id=(gx, (gy + s) % ny), device_id_type=MESH)
    for px in (up, down):
        for py in (left, right):
            pl.semaphore_signal(barrier, inc=1, device_id=(px, py), device_id_type=MESH)

    lane = lax.broadcasted_iota(jnp.int32, (EXT, T), 1)
    row = lax.broadcasted_iota(jnp.int32, (EXT, T), 0)
    xpos = gx * T - 8 + row
    in_x = (xpos >= 0) & (xpos < full_x)
    dist_x = plane_dist(
        xpos.astype(jnp.float32), sp_ref[1].astype(jnp.float32), an_ref[1].astype(jnp.float32)
    )
    for part in range(2):
        if part == 0:
            ypos = gy * T + lane
            keep = in_x
        else:
            ypos = gy * T + jnp.where(lane < T // 2, lane + T, lane - T)
            keep = in_x & (ypos >= 0) & (ypos < full_y) & ((lane < 4) | (lane >= T - 4))
        dist_y = plane_dist(
            ypos.astype(jnp.float32), sp_ref[2].astype(jnp.float32), an_ref[2].astype(jnp.float32)
        )
        hole = dist_x * dist_x + dist_y * dist_y <= re_ref[0].astype(jnp.float32)
        inside[part] = jnp.where(keep, 1.0, 0.0)
        flat[part] = jnp.where(keep & hole, 1.0, 0.0)

    sub = lax.broadcasted_iota(jnp.int32, (8, T), 0)
    group = lax.broadcasted_iota(jnp.int32, (T, T), 1) // 4
    first = second = jnp.zeros((T, T), jnp.float32)
    for arr, src in enumerate((iv, wv)):
        loads[arr].wait()
        ends = []
        for slot in range(slots):
            layer = an_ref[0] + (slot // 3) * sp_ref[0] + (slot % 3 - 1)
            tile = src[jnp.clip(layer, 0, depth - 1)]
            place = slot + arr * slots
            first = jnp.where(group == place, pltpu.roll(tile, (4 * place + 4) % T, 1), first)
            second = jnp.where(group == place, pltpu.roll(tile, (4 * place) % T, 1), second)
            ends.append((tile[0:8], tile[T - 8 : T]))
        for pair in range(slots // 2):
            even, odd = ends[2 * pair], ends[2 * pair + 1]
            xpack[0, arr, pair] = jnp.where(sub < 4, even[0], pltpu.roll(odd[0], 4, 0))
            xpack[1, arr, pair] = jnp.where(sub >= 4, even[1], pltpu.roll(odd[1], 4, 0))
    ypack[0] = first
    ypack[1] = second

    pl.semaphore_wait(barrier, (nx - 1) + (ny - 1) + 4)

    has_up, has_down = gx > 0, gx < nx - 1
    has_left, has_right = gy > 0, gy < ny - 1
    ends, starts, rows = pl.ds(T - 8, 8), pl.ds(0, 8), pl.ds(8, T)
    before, after = pl.ds(0, 8), pl.ds(T + 8, 8)
    routes = (
        (ypack.at[0], yrecv.at[0, rows], (gx, right), has_right, has_left),
        (ypack.at[1], yrecv.at[1, rows], (gx, left), has_left, has_right),
        (xpack.at[0], xrecv.at[1], (up, gy), has_up, has_down),
        (xpack.at[1], xrecv.at[0], (down, gy), has_down, has_up),
        (ypack.at[0, ends], yrecv.at[0, before], (down, right), has_down & has_right, has_up & has_left),
        (ypack.at[0, starts], yrecv.at[0, after], (up, right), has_up & has_right, has_down & has_left),
        (ypack.at[1, ends], yrecv.at[1, before], (down, left), has_down & has_left, has_up & has_right),
        (ypack.at[1, starts], yrecv.at[1, after], (up, left), has_up & has_left, has_down & has_right),
    )
    halo = []
    for i, (src, dst, dev, sends, receives) in enumerate(routes):
        cp = pltpu.make_async_remote_copy(
            src_ref=src, dst_ref=dst, send_sem=hs.at[i], recv_sem=hr.at[i],
            device_id=dev, device_id_type=MESH,
        )
        halo.append((cp, sends, receives))
        pl.when(sends)(cp.start)
    for cp in consts:
        cp.start()
    for cp, _, receives in halo:
        pl.when(receives)(cp.wait_recv)

    def blur(main, side):
        def across(a, b):
            before = pltpu.roll(jnp.where(lane == T - 1, b, a), 1, 1)
            after = pltpu.roll(jnp.where(lane == 0, b, a), T - 1, 1)
            s = (before + after) + (a + a)
            return (pltpu.roll(s, 1, 0) + pltpu.roll(s, EXT - 1, 0)) + (s + s)

        return across(main, side), across(side, main)

    def extended(arr, src, layer, slot):
        top, bottom = xrecv[0, arr, slot // 2], xrecv[1, arr, slot // 2]
        odd = jnp.full((8, T), slot % 2, jnp.int32) == 1
        top = jnp.where(odd, pltpu.roll(top, 4, 0), top)
        bottom = jnp.where(odd, pltpu.roll(bottom, 4, 0), bottom)
        main = jnp.concatenate([top, src[layer], bottom], axis=0)
        shift = 2 * T - 4 * (slot + arr * slots)
        before = pltpu.roll(yrecv[0], (shift - 4) % T, 1)
        after = pltpu.roll(yrecv[1], shift % T, 1)
        return main, jnp.where(lane < T // 2, after, before)

    def fill(layer):
        place = layer - an_ref[0] + 1
        turn = 0
        for m in range(1, slots // 3):
            turn = turn + (place >= m * sp_ref[0]).astype(jnp.int32)
        slot = 3 * turn + jnp.clip(place - turn * sp_ref[0], 0, 2)
        zpos = lax.broadcasted_iota(jnp.int32, (1, T), 0) + layer
        dist_z = plane_dist(
            zpos.astype(jnp.float32), sp_ref[0].astype(jnp.float32), an_ref[0].astype(jnp.float32)
        )
        zflag = jnp.where(dist_z <= 1.0, 1.0, 0.0)
        masks = [flat[part] * zflag for part in range(2)]
        holes = [m > 0.5 for m in masks]
        weights = [
            jnp.where(inside[part] > 0.5, w, 0.0)
            for part, w in enumerate(extended(1, wv, layer, slot))
        ]
        values = [
            jnp.where(inside[part] - masks[part] > 0.5, v, 0.0)
            for part, v in enumerate(extended(0, iv, layer, slot))
        ]
        inverse = [
            1.0 / jnp.where(h, d, 1.0) for h, d in zip(holes, blur(*weights))
        ]
        for _ in range(3):
            numer = blur(*[w * v for w, v in zip(weights, values)])
            values = [
                jnp.where(h, n * r, v) for h, n, r, v in zip(holes, numer, inverse, values)
            ]
        fbuf[layer] = values[0][8 : 8 + T]

    def first_copy(layer, half, peer):
        return pltpu.make_async_remote_copy(
            src_ref=fbuf.at[layer], dst_ref=recv1.at[gx, half],
            send_sem=s1.at[layer], recv_sem=r1.at[gx, half],
            device_id=(peer, gy), device_id_type=MESH,
        )

    for half in range(2):
        @pl.loop(0, nx - 1)
        def _(t):
            peer = xor(gx, nx - 1 - t, bits_x)
            layer = 2 * peer + half
            fill(layer)
            first_copy(layer, half, peer).start()

    for half in range(2):
        fill(2 * gx + half)
        recv1[gx, half] = fbuf[2 * gx + half]

    def second_copy(half, block):
        return pltpu.make_async_remote_copy(
            src_ref=sbuf.at[half, block], dst_ref=recv2.at[gy, half],
            send_sem=s2.at[half, block], recv_sem=r2.at[gy, half],
            device_id=(gx, block), device_id_type=MESH,
        )

    groups = ny // 4
    order = [o for o in (2, 3, 1, 0) if o < groups]
    for half in range(2):
        @pl.loop(0, nx)
        def _(t):
            peer = xor(gx, t, bits_x)

            @pl.when(t > 0)
            def _():
                pltpu.make_async_remote_copy(
                    src_ref=fbuf.at[0], dst_ref=recv1.at[peer, half],
                    send_sem=s1.at[0], recv_sem=r1.at[peer, half],
                    device_id=(peer, gy), device_id_type=MESH,
                ).wait_recv()

            high, low = high_low(recv1[peer, half])
            start = pl.multiple_of(peer * T, T)
            fx[pl.ds(start, T), 0:T] = high
            fx[pl.ds(start, T), T : 2 * T] = low

        if half == 0:
            for cp in consts[:2]:
                cp.wait()
        for o in order:
            group = xor(gy // 4, o, bits_y - 2)
            start = pl.multiple_of(group * (4 * T), 4 * T)
            both = jnp.dot(
                chi[pl.ds(start, 4 * T), :], fx[...], preferred_element_type=jnp.float32
            )
            rest = jnp.dot(
                clo[pl.ds(start, 4 * T), :], fx[:, 0:T], preferred_element_type=jnp.float32
            )
            total = both[:, 0:T] + (both[:, T : 2 * T] + rest)
            for j in range(4):
                sbuf[half, 4 * group + j] = total[j * T : (j + 1) * T]
            for j in range(4):
                block = 4 * group + xor(gy % 4, j, 2)

                @pl.when(block != gy)
                def _():
                    second_copy(half, block).start()

                @pl.when(block == gy)
                def _():
                    recv2[gy, half] = sbuf[half, block]

    for cp in consts[2:]:
        cp.wait()
    for half in range(2):
        for o in range(groups):
            group = xor(gy // 4, o, bits_y - 2)
            parts = []
            for j in range(4):
                block = 4 * group + j

                @pl.when(block != gy)
                def _():
                    pltpu.make_async_remote_copy(
                        src_ref=sbuf.at[half, 0], dst_ref=recv2.at[block, half],
                        send_sem=s2.at[half, 0], recv_sem=r2.at[block, half],
                        device_id=(gx, block), device_id_type=MESH,
                    ).wait_recv()

                parts.append(recv2[block, half])
            high, low = high_low(jnp.concatenate(parts, axis=1))
            stacked = jnp.concatenate([high, low], axis=0)
            start = pl.multiple_of(group * (4 * T), 4 * T)

            @pl.loop(0, full_y // 512)
            def _(c):
                cols = pl.ds(pl.multiple_of(c * 512, 512), 512)
                both = jnp.dot(
                    stacked, thi[pl.ds(start, 4 * T), cols], preferred_element_type=jnp.float32
                )
                rest = jnp.dot(
                    high, tlo[pl.ds(start, 4 * T), cols], preferred_element_type=jnp.float32
                )
                total = both[0:T] + (both[T : 2 * T] + rest)
                if o == 0:
                    acc[half, :, cols] = total
                else:
                    acc[half, :, cols] += total


    for half in range(2):
        @pl.loop(0, nx - 1)
        def _(t):
            peer = xor(gx, nx - 1 - t, bits_x)
            first_copy(2 * peer + half, half, peer).wait_send()

        @pl.loop(1, ny)
        def _(t):
            second_copy(half, xor(gy, t, bits_y)).wait_send()
    for cp, sends, _ in halo:
        pl.when(sends)(cp.wait_send)


def per_device(nx, ny, intensity, weight, spacing, anchor, reach):
    depth = intensity.shape[0]
    full_x, full_y = nx * T, ny * T
    chi, clo = split_pair(cosine_matrix(full_x))
    thi, tlo = split_pair(cosine_matrix(full_y).T)
    f32, bf16 = jnp.float32, jnp.bfloat16
    vmem, dma = pltpu.VMEM, pltpu.SemaphoreType.DMA
    anywhere = pl.BlockSpec(memory_space=pl.ANY)
    scalars = pl.BlockSpec(memory_space=pltpu.SMEM)
    slots = hole_slots(depth)
    return pl.pallas_call(
        functools.partial(kernel, nx, ny, depth),
        out_shape=pltpu.VMEM((2, T, full_y), f32),
        in_specs=[anywhere] * 2 + [scalars] * 3 + [anywhere] * 4,
        out_specs=pl.BlockSpec(memory_space=pltpu.VMEM),
        scratch_shapes=[
            vmem((depth, T, T), f32),
            vmem((depth, T, T), f32),
            vmem((depth, T, T), f32),
            vmem((2, 2, slots // 2, 8, T), f32),
            vmem((2, 2, slots // 2, 8, T), f32),
            vmem((2, T, T), f32),
            vmem((2, EXT, T), f32),
            vmem((2, EXT, T), f32),
            vmem((2, EXT, T), f32),
            vmem((nx, 2, T, T), f32),
            vmem((full_x, 2 * T), bf16),
            vmem((2, ny, T, T), f32),
            vmem((ny, 2, T, T), f32),
            vmem((full_x, full_x), bf16),
            vmem((full_x, full_x), bf16),
            vmem((full_y, full_y), bf16),
            vmem((full_y, full_y), bf16),
            dma((2,)), dma((4,)), dma((8,)), dma((8,)),
            dma((depth,)), dma((nx, 2)), dma((2, ny)), dma((ny, 2)),
        ],
        compiler_params=pltpu.CompilerParams(
            collective_id=0, has_side_effects=True, vmem_limit_bytes=54 * 2**20
        ),
    )(intensity, weight, spacing, anchor, reach, chi, clo, thi, tlo)


def solution(mesh):
    nx, ny = mesh.shape["gx"], mesh.shape["gy"]
    in_specs = (P(None, "gx", "gy"), P(None, "gx", "gy"), P(), P(), P())
    return jax.shard_map(
        functools.partial(per_device, nx, ny),
        mesh=mesh, in_specs=in_specs, out_specs=P("gx", "gy", None), check_vma=False,
    )
```

```python
import functools

import jax
import jax.numpy as jnp
import ml_dtypes
import numpy as np
from jax import lax
from jax.experimental import pallas as pl
from jax.experimental.pallas import tpu as pltpu
from jax.sharding import PartitionSpec as P

MESH = pl.DeviceIdType.MESH
T = 128
EXT = T + 16


def cosine_matrix(length):
    k = np.arange(length, dtype=np.int64)
    phase = (k[:, None] * (2 * k[None, :] + 1)) % (4 * length)
    return np.cos(phase * (np.pi / (2 * length))) * np.sqrt(2.0 / length)


def split_pair(matrix):
    matrix = matrix.astype(np.float32)
    high = matrix.astype(ml_dtypes.bfloat16)
    low = (matrix - high.astype(np.float32)).astype(ml_dtypes.bfloat16)
    return high, low


def xor(a, b, bits):
    total = 0
    for i in range(bits):
        total = total + (2**i) * ((a // 2**i + b // 2**i) % 2)
    return total


def high_low(x):
    high = x.astype(jnp.bfloat16)
    return high, (x - high.astype(jnp.float32)).astype(jnp.bfloat16)


def plane_dist(position, spacing, anchor):
    offset = position - anchor
    offset = offset - spacing * jnp.floor((offset + 0.5) / spacing)
    return jnp.minimum(offset, spacing - offset)


def hole_slots(depth):
    return 3 * (depth // 10 + 1) + 3 * (depth // 10 + 1) % 2


def kernel(
    nx, ny, depth,
    i_hbm, w_hbm, sp_ref, an_ref, re_ref, chi_hbm, clo_hbm, thi_hbm, tlo_hbm,
    acc,
    iv, wv, fbuf, xpack, xrecv, ypack, yrecv, flat, inside,
    recv1, fx, sbuf, recv2, chi, clo, thi, tlo,
    lsem, csem, hs, hr, s1, r1, s2, r2,
):
    gx = lax.axis_index("gx")
    gy = lax.axis_index("gy")
    full_x, full_y = nx * T, ny * T
    slots = hole_slots(depth)
    bits_x, bits_y = nx.bit_length() - 1, ny.bit_length() - 1
    left, right = (gy + ny - 1) % ny, (gy + 1) % ny
    up, down = (gx + nx - 1) % nx, (gx + 1) % nx

    loads = [
        pltpu.make_async_copy(i_hbm, iv, lsem.at[0]),
        pltpu.make_async_copy(w_hbm, wv, lsem.at[1]),
    ]
    consts = [
        pltpu.make_async_copy(src, dst, csem.at[i])
        for i, (src, dst) in enumerate(
            ((chi_hbm, chi), (clo_hbm, clo), (thi_hbm, thi), (tlo_hbm, tlo))
        )
    ]
    for cp in loads:
        cp.start()
    barrier = pltpu.get_barrier_semaphore()
    for s in range(1, nx):
        pl.semaphore_signal(barrier, inc=1, device_id=((gx + s) % nx, gy), device_id_type=MESH)
    for s in range(1, ny):
        pl.semaphore_signal(barrier, inc=1, device_id=(gx, (gy + s) % ny), device_id_type=MESH)
    for px in (up, down):
        for py in (left, right):
            pl.semaphore_signal(barrier, inc=1, device_id=(px, py), device_id_type=MESH)

    lane = lax.broadcasted_iota(jnp.int32, (EXT, T), 1)
    row = lax.broadcasted_iota(jnp.int32, (EXT, T), 0)
    xpos = gx * T - 8 + row
    in_x = (xpos >= 0) & (xpos < full_x)
    dist_x = plane_dist(
        xpos.astype(jnp.float32), sp_ref[1].astype(jnp.float32), an_ref[1].astype(jnp.float32)
    )
    for part in range(2):
        if part == 0:
            ypos = gy * T + lane
            keep = in_x
        else:
            ypos = gy * T + jnp.where(lane < T // 2, lane + T, lane - T)
            keep = in_x & (ypos >= 0) & (ypos < full_y) & ((lane < 4) | (lane >= T - 4))
        dist_y = plane_dist(
            ypos.astype(jnp.float32), sp_ref[2].astype(jnp.float32), an_ref[2].astype(jnp.float32)
        )
        hole = dist_x * dist_x + dist_y * dist_y <= re_ref[0].astype(jnp.float32)
        inside[part] = jnp.where(keep, 1.0, 0.0)
        flat[part] = jnp.where(keep & hole, 1.0, 0.0)

    sub = lax.broadcasted_iota(jnp.int32, (8, T), 0)
    group = lax.broadcasted_iota(jnp.int32, (T, T), 1) // 4
    first = second = jnp.zeros((T, T), jnp.float32)
    for arr, src in enumerate((iv, wv)):
        loads[arr].wait()
        ends = []
        for slot in range(slots):
            layer = an_ref[0] + (slot // 3) * sp_ref[0] + (slot % 3 - 1)
            tile = src[jnp.clip(layer, 0, depth - 1)]
            place = slot + arr * slots
            first = jnp.where(group == place, pltpu.roll(tile, (4 * place + 4) % T, 1), first)
            second = jnp.where(group == place, pltpu.roll(tile, (4 * place) % T, 1), second)
            ends.append((tile[0:8], tile[T - 8 : T]))
        for pair in range(slots // 2):
            even, odd = ends[2 * pair], ends[2 * pair + 1]
            xpack[0, arr, pair] = jnp.where(sub < 4, even[0], pltpu.roll(odd[0], 4, 0))
            xpack[1, arr, pair] = jnp.where(sub >= 4, even[1], pltpu.roll(odd[1], 4, 0))
    ypack[0] = first
    ypack[1] = second

    pl.semaphore_wait(barrier, (nx - 1) + (ny - 1) + 4)

    has_up, has_down = gx > 0, gx < nx - 1
    has_left, has_right = gy > 0, gy < ny - 1
    ends, starts, rows = pl.ds(T - 8, 8), pl.ds(0, 8), pl.ds(8, T)
    before, after = pl.ds(0, 8), pl.ds(T + 8, 8)
    routes = (
        (ypack.at[0], yrecv.at[0, rows], (gx, right), has_right, has_left),
        (ypack.at[1], yrecv.at[1, rows], (gx, left), has_left, has_right),
        (xpack.at[0], xrecv.at[1], (up, gy), has_up, has_down),
        (xpack.at[1], xrecv.at[0], (down, gy), has_down, has_up),
        (ypack.at[0, ends], yrecv.at[0, before], (down, right), has_down & has_right, has_up & has_left),
        (ypack.at[0, starts], yrecv.at[0, after], (up, right), has_up & has_right, has_down & has_left),
        (ypack.at[1, ends], yrecv.at[1, before], (down, left), has_down & has_left, has_up & has_right),
        (ypack.at[1, starts], yrecv.at[1, after], (up, left), has_up & has_left, has_down & has_right),
    )
    halo = []
    for i, (src, dst, dev, sends, receives) in enumerate(routes):
        cp = pltpu.make_async_remote_copy(
            src_ref=src, dst_ref=dst, send_sem=hs.at[i], recv_sem=hr.at[i],
            device_id=dev, device_id_type=MESH,
        )
        halo.append((cp, sends, receives))
        pl.when(sends)(cp.start)
    for cp in consts:
        cp.start()
    for cp, _, receives in halo:
        pl.when(receives)(cp.wait_recv)

    def blur(main, side):
        def across(a, b):
            before = pltpu.roll(jnp.where(lane == T - 1, b, a), 1, 1)
            after = pltpu.roll(jnp.where(lane == 0, b, a), T - 1, 1)
            s = (before + after) + (a + a)
            return (pltpu.roll(s, 1, 0) + pltpu.roll(s, EXT - 1, 0)) + (s + s)

        return across(main, side), across(side, main)

    def extended(arr, src, layer, slot):
        top, bottom = xrecv[0, arr, slot // 2], xrecv[1, arr, slot // 2]
        odd = jnp.full((8, T), slot % 2, jnp.int32) == 1
        top = jnp.where(odd, pltpu.roll(top, 4, 0), top)
        bottom = jnp.where(odd, pltpu.roll(bottom, 4, 0), bottom)
        main = jnp.concatenate([top, src[layer], bottom], axis=0)
        shift = 2 * T - 4 * (slot + arr * slots)
        before = pltpu.roll(yrecv[0], (shift - 4) % T, 1)
        after = pltpu.roll(yrecv[1], shift % T, 1)
        return main, jnp.where(lane < T // 2, after, before)

    def fill(layer):
        place = layer - an_ref[0] + 1
        turn = 0
        for m in range(1, slots // 3):
            turn = turn + (place >= m * sp_ref[0]).astype(jnp.int32)
        slot = 3 * turn + jnp.clip(place - turn * sp_ref[0], 0, 2)
        zpos = lax.broadcasted_iota(jnp.int32, (1, T), 0) + layer
        dist_z = plane_dist(
            zpos.astype(jnp.float32), sp_ref[0].astype(jnp.float32), an_ref[0].astype(jnp.float32)
        )
        zflag = jnp.where(dist_z <= 1.0, 1.0, 0.0)
        masks = [flat[part] * zflag for part in range(2)]
        holes = [m > 0.5 for m in masks]
        weights = [
            jnp.where(inside[part] > 0.5, w, 0.0)
            for part, w in enumerate(extended(1, wv, layer, slot))
        ]
        values = [
            jnp.where(inside[part] - masks[part] > 0.5, v, 0.0)
            for part, v in enumerate(extended(0, iv, layer, slot))
        ]
        inverse = [
            1.0 / jnp.where(h, d, 1.0) for h, d in zip(holes, blur(*weights))
        ]
        for _ in range(3):
            numer = blur(*[w * v for w, v in zip(weights, values)])
            values = [
                jnp.where(h, n * r, v) for h, n, r, v in zip(holes, numer, inverse, values)
            ]
        fbuf[layer] = values[0][8 : 8 + T]

    def first_copy(layer, half, peer):
        return pltpu.make_async_remote_copy(
            src_ref=fbuf.at[layer], dst_ref=recv1.at[gx, half],
            send_sem=s1.at[layer], recv_sem=r1.at[gx, half],
            device_id=(peer, gy), device_id_type=MESH,
        )

    for half in range(2):
        @pl.loop(0, nx - 1)
        def _(t):
            peer = xor(gx, nx - 1 - t, bits_x)
            layer = 2 * peer + half
            fill(layer)

            if half == 1:
                first_copy(layer - 1, 0, peer).wait_send()
            first_copy(layer, half, peer).start()

        if half == 0:
            for own in range(2):
                fill(2 * gx + own)
                recv1[gx, own] = fbuf[2 * gx + own]

    def second_copy(half, block):
        return pltpu.make_async_remote_copy(
            src_ref=sbuf.at[half, block], dst_ref=recv2.at[gy, half],
            send_sem=s2.at[half, block], recv_sem=r2.at[gy, half],
            device_id=(gx, block), device_id_type=MESH,
        )

    def start_group(half, group):
        for j in range(4):
            block = 4 * group + xor(gy % 4, j, 2)

            @pl.when(block != gy)
            def _():
                second_copy(half, block).start()

            @pl.when(block == gy)
            def _():
                recv2[gy, half] = sbuf[half, gy]

    groups = ny // 4
    late = min(3, groups - 1)
    order = [o for o in (2, 3, 1, 0) if o < groups]
    for half in range(2):
        @pl.loop(0, nx)
        def _(t):
            peer = xor(gx, t, bits_x)

            @pl.when(t > 0)
            def _():
                pltpu.make_async_remote_copy(
                    src_ref=fbuf.at[0], dst_ref=recv1.at[peer, half],
                    send_sem=s1.at[0], recv_sem=r1.at[peer, half],
                    device_id=(peer, gy), device_id_type=MESH,
                ).wait_recv()

            if half == 1:
                @pl.when(t == nx - 2)
                def _():
                    start_group(0, xor(gy // 4, late, bits_y - 2))

            high, low = high_low(recv1[peer, half])
            start = pl.multiple_of(peer * T, T)
            fx[pl.ds(start, T), 0:T] = high
            fx[pl.ds(start, T), T : 2 * T] = low

        if half == 0:
            for cp in consts[:2]:
                cp.wait()
        for o in order:
            group = xor(gy // 4, o, bits_y - 2)
            start = pl.multiple_of(group * (4 * T), 4 * T)
            both = jnp.dot(
                chi[pl.ds(start, 4 * T), :], fx[...], preferred_element_type=jnp.float32
            )
            rest = jnp.dot(
                clo[pl.ds(start, 4 * T), :], fx[:, 0:T], preferred_element_type=jnp.float32
            )
            total = both[:, 0:T] + (both[:, T : 2 * T] + rest)
            for j in range(4):
                sbuf[half, 4 * group + j] = total[j * T : (j + 1) * T]
            if half == 1 or o != late:
                start_group(half, group)

    for cp in consts[2:]:
        cp.wait()
    for half in range(2):
        steps = [(o, 0, 4) for o in range(groups)]
        if half == 1:
            steps[-1:] = [(groups - 1, 0, 2), (groups - 1, 1, 2)]
        for o, part, count in steps:
            first = 4 * xor(gy // 4, o, bits_y - 2)
            if count == 2:
                first = first + 2 * xor(gy % 4 // 2, part, 1)
            parts = []
            for j in range(count):
                block = first + j

                @pl.when(block != gy)
                def _():
                    pltpu.make_async_remote_copy(
                        src_ref=sbuf.at[half, 0], dst_ref=recv2.at[block, half],
                        send_sem=s2.at[half, 0], recv_sem=r2.at[block, half],
                        device_id=(gx, block), device_id_type=MESH,
                    ).wait_recv()

                parts.append(recv2[block, half])
            high, low = high_low(jnp.concatenate(parts, axis=1))
            stacked = jnp.concatenate([high, low], axis=0)
            rows = pl.ds(pl.multiple_of(first * T, count * T), count * T)

            @pl.loop(0, full_y // 512)
            def _(c):
                cols = pl.ds(pl.multiple_of(c * 512, 512), 512)
                both = jnp.dot(
                    stacked, thi[rows, cols], preferred_element_type=jnp.float32
                )
                rest = jnp.dot(
                    high, tlo[rows, cols], preferred_element_type=jnp.float32
                )
                total = both[0:T] + (both[T : 2 * T] + rest)
                if o == 0 and part == 0:
                    acc[half, :, cols] = total
                else:
                    acc[half, :, cols] += total


    for half in range(2):
        if half == 1:
            @pl.loop(0, nx - 1)
            def _(t):
                peer = xor(gx, nx - 1 - t, bits_x)
                first_copy(2 * peer + half, half, peer).wait_send()

        @pl.loop(1, ny)
        def _(t):
            second_copy(half, xor(gy, t, bits_y)).wait_send()
    for cp, sends, _ in halo:
        pl.when(sends)(cp.wait_send)


def per_device(nx, ny, intensity, weight, spacing, anchor, reach):
    depth = intensity.shape[0]
    full_x, full_y = nx * T, ny * T
    chi, clo = split_pair(cosine_matrix(full_x))
    thi, tlo = split_pair(cosine_matrix(full_y).T)
    f32, bf16 = jnp.float32, jnp.bfloat16
    vmem, dma = pltpu.VMEM, pltpu.SemaphoreType.DMA
    anywhere = pl.BlockSpec(memory_space=pl.ANY)
    scalars = pl.BlockSpec(memory_space=pltpu.SMEM)
    slots = hole_slots(depth)
    return pl.pallas_call(
        functools.partial(kernel, nx, ny, depth),
        out_shape=pltpu.VMEM((2, T, full_y), f32),
        in_specs=[anywhere] * 2 + [scalars] * 3 + [anywhere] * 4,
        out_specs=pl.BlockSpec(memory_space=pltpu.VMEM),
        scratch_shapes=[
            vmem((depth, T, T), f32),
            vmem((depth, T, T), f32),
            vmem((depth, T, T), f32),
            vmem((2, 2, slots // 2, 8, T), f32),
            vmem((2, 2, slots // 2, 8, T), f32),
            vmem((2, T, T), f32),
            vmem((2, EXT, T), f32),
            vmem((2, EXT, T), f32),
            vmem((2, EXT, T), f32),
            vmem((nx, 2, T, T), f32),
            vmem((full_x, 2 * T), bf16),
            vmem((2, ny, T, T), f32),
            vmem((ny, 2, T, T), f32),
            vmem((full_x, full_x), bf16),
            vmem((full_x, full_x), bf16),
            vmem((full_y, full_y), bf16),
            vmem((full_y, full_y), bf16),
            dma((2,)), dma((4,)), dma((8,)), dma((8,)),
            dma((depth,)), dma((nx, 2)), dma((2, ny)), dma((ny, 2)),
        ],
        compiler_params=pltpu.CompilerParams(
            collective_id=0, has_side_effects=True, vmem_limit_bytes=54 * 2**20
        ),
    )(intensity, weight, spacing, anchor, reach, chi, clo, thi, tlo)


def solution(mesh):
    nx, ny = mesh.shape["gx"], mesh.shape["gy"]
    in_specs = (P(None, "gx", "gy"), P(None, "gx", "gy"), P(), P(), P())
    return jax.shard_map(
        functools.partial(per_device, nx, ny),
        mesh=mesh, in_specs=in_specs, out_specs=P("gx", "gy", None), check_vma=False,
    )
```
